256 devices in a mesh: dp: 64 (over x, z, core), fsdp: 4 (over y).
Axes of the slice: x: 4, y: 4, z: 8, core: 2. Of those that a mesh axis runs over, the one named last changes fastest.
Arguments:
- acts: bfloat16 [131072, 4096], P(('dp', 'fsdp')), may hold values from -6 to 6
- cotangent: bfloat16 [131072, 512], P(('dp', 'fsdp')), may hold values from -6 to 6
- weight: bfloat16 [4096, 512], P('fsdp'), may hold values from -0.09375 to 0.09375
- error_buf: float32 [64, 4096, 512], P('dp', 'fsdp'), may hold values from -100 to 100, as said below
- q_init: float32 [512, 64], replicated, may hold values from -6 to 6
- inv_scale: float32 [], replicated, may hold values from 0.011048543 to 0.022097087
Outputs:
- input_grad: bfloat16 [131072, 4096], P(('dp', 'fsdp'))
- approx: float32 [4096, 512], P('fsdp')
- new_error: float32 [64, 4096, 512], P('dp', 'fsdp')
- q_next: float32 [512, 64], replicated
The draws below stay inside these ranges and needn't reach their ends.
Inputs may be any that keep to these rules, and one draw needn't show every extreme that they name: `error_buf`: error feedback carried from the previous step.
All inputs are finite; a program needn't handle non-finite values.
Results may differ from the reference program's by a relative error of at most 0.0033.
Values may be sent and summed in bfloat16 or wider, within the bound.
No kernel may reach another device: no remote copies, remote signals or barrier semaphores. Data moves between devices by JAX's collectives and lax.ppermute only.
A program may use at most 64 MiB of HBM per device.

```python
import math
import jax
import jax.numpy as jnp
from jax import lax

D = 4096
KVC = 512
R = 64
ITERS = 2
TOK_DEV = 512
TOKENS = 131072
N_DP = 64
N_FSDP = 4


def draw_error_buf(key, part):
    key_common = jax.random.fold_in(key, 11)
    key_own = jax.random.fold_in(key, 12)
    key_level = jax.random.fold_in(key, 13)
    common = jax.random.truncated_normal(key_common, -4.0, 4.0, (D, KVC), jnp.float32)
    own = jax.random.truncated_normal(key_own, -4.0, 4.0, (N_DP, D, KVC), jnp.float32)
    level = jax.random.uniform(key_level, (D, 1), jnp.float32)
    rise = jnp.arange(D, dtype=jnp.float32)[:, None] / (D - 1)
    row_scale = jnp.exp(math.log(10.0) * level + math.log(3.0) * rise)
    base = common[None] + own
    return base * row_scale[None] / 6.0


def block_levels(rng, extent, split, least, top_value):
    gain, own = 1.0, jax.random.fold_in(rng, 6)
    for position, shards_of in split:
        steps = jnp.exp(jax.random.uniform(jax.random.fold_in(own, position), (shards_of,), jnp.float32, least / len(split), top_value / len(split)))
        gain = gain * jnp.repeat(steps, extent[position] // shards_of).reshape([-1 if axis == position else 1 for axis in range(len(extent))])
    return gain


def normal_values(key, shape, spread, limit, cuts=(), held_as=jnp.bfloat16):
    array = jax.random.normal(key, shape, jnp.float32) * spread
    if len(cuts) > 0:
        array = block_levels(key, shape, cuts, -0.22, 0.18) * array
    return jnp.clip(array, min=-limit, max=limit).astype(held_as)


def setup_inputs(seed: int = 0) -> dict:
    splits = jax.random.split(jax.random.key(seed), 7)
    acts = normal_values(splits[0], (TOKENS, D), 1.0, 6.0, ((0, 256),))
    cotangent = normal_values(splits[1], (TOKENS, KVC), 1.0, 6.0, ((0, 256),))
    weight = normal_values(splits[2], (D, KVC), D ** -0.5, 0.09375, ((0, 4),))
    error_buf = draw_error_buf(jax.random.fold_in(splits[6], 71), 0)
    q_init = normal_values(splits[4], (KVC, R), 1.0, 6.0, (), jnp.float32)
    inv_scale = jnp.clip(jnp.exp(jax.random.uniform(splits[5], (), jnp.float32, math.log(0.011048543), math.log(0.022097087))), 0.011048543, 0.022097087)
    return dict(acts=acts, cotangent=cotangent, weight=weight, error_buf=error_buf, q_init=q_init, inv_scale=inv_scale)


def orthonormal(factor):
    gram = jnp.dot(factor.T, factor, precision=lax.Precision.HIGHEST)
    lower = jnp.linalg.cholesky(gram)
    return lax.linalg.triangular_solve(lower, factor, left_side=False, lower=True, transpose_a=True)

def reference(acts, cotangent, weight, error_buf, q_init, inv_scale):
    input_grad = jnp.dot(cotangent.astype(jnp.float32), weight.T.astype(jnp.float32), preferred_element_type=jnp.float32).astype(jnp.bfloat16)
    group = TOK_DEV * N_FSDP
    acts_three = acts.reshape(N_DP, group, D)
    cot_three = cotangent.reshape(N_DP, group, KVC)

    def replica_grad(pair):
        return jnp.dot(pair[0].T.astype(jnp.float32), pair[1].astype(jnp.float32), preferred_element_type=jnp.float32)
    grads = lax.map(replica_grad, (acts_three, cot_three))
    merged = error_buf + inv_scale * grads
    mean_merged = lax.optimization_barrier(jnp.sum(merged, axis=0)) / N_DP
    factor_q = q_init
    p_hat = None
    for step in range(ITERS):
        factor_p = jnp.dot(mean_merged, factor_q, precision=lax.Precision.HIGHEST)
        p_hat = orthonormal(factor_p)
        factor_q = jnp.dot(mean_merged.T, p_hat, precision=lax.Precision.HIGHEST)
    approx = jnp.dot(p_hat, factor_q.T, precision=lax.Precision.HIGHEST)
    new_error = merged - approx[None]
    return (input_grad, approx, new_error, factor_q)
```

```python
import jax
import jax.numpy as jnp
from jax import lax
from jax.sharding import Mesh
from jax.sharding import PartitionSpec as P

ITERS = 2
NX, NZ, NC, NY = 4, 8, 2, 4
DP = ("x", "z", "core")
HI = lax.Precision.HIGHEST
f32, bf16 = jnp.float32, jnp.bfloat16
SWAP = [(0, 1), (1, 0)]


def dot(a, b, dims):
    return lax.dot_general(a, b, (dims, ((), ())), precision=HI, preferred_element_type=f32)


def gather_weight(weight, y, core):
    half = lax.dynamic_slice_in_dim(weight, core * 512, 512, 0)
    pieces = [half]
    for s in range(1, NY):
        pieces.append(lax.ppermute(half, "y", [(i, (i + s) % NY) for i in range(NY)]))
    mine = lax.concatenate([pieces[s] for s in (3, 2, 1, 0, 3, 2, 1)], 0)
    mine = lax.dynamic_slice_in_dim(mine, (NY - 1 - y) * 512, NY * 512, 0).reshape(NY, 512, 512)
    other = lax.ppermute(mine, "core", SWAP)
    low = jnp.where(core == 0, mine, other)
    high = jnp.where(core == 0, other, mine)
    return jnp.stack([low, high], axis=1).reshape(NY * 1024, 512)


def sum_y(t):
    got = lax.all_to_all(jnp.broadcast_to(t, (NY, *t.shape)), "y", 0, 0, tiled=True)
    return (got[0] + got[1]) + (got[2] + got[3])


def body(acts, cotangent, weight, error_buf, q_init, inv_scale):
    y, core = lax.axis_index("y"), lax.axis_index("core")
    part = jnp.einsum("tr,tk->rk", acts, cotangent, preferred_element_type=f32).astype(bf16)
    recv = lax.all_to_all(part.reshape(NY, 1024, 512), "y", 0, 0, tiled=True)
    recv, weight = lax.optimization_barrier((recv, weight))
    full_weight = gather_weight(weight, y, core)
    input_grad = jnp.einsum("tk,rk->tr", cotangent, full_weight, preferred_element_type=f32).astype(bf16)

    merged = error_buf[0] + inv_scale * jnp.sum(recv.astype(f32), axis=0)
    keep = lax.dynamic_slice_in_dim(merged, core * 512, 512, 0)
    give = lax.dynamic_slice_in_dim(merged, (1 - core) * 512, 512, 0).astype(bf16)
    pair = keep + lax.ppermute(give, "core", SWAP).astype(f32)
    terms = lax.all_to_all(pair.astype(bf16).reshape(NX * NZ, 16, 512), ("x", "z"), 0, 0, tiled=True)
    rows = jnp.sum(terms.astype(f32), axis=0) * (1.0 / (NX * NZ * NC))
    half = lax.all_to_all(jnp.broadcast_to(rows, (NX * NZ, 16, 512)), ("x", "z"), 0, 0, tiled=True)
    half = half.reshape(512, 512)
    other = lax.ppermute(half, "core", SWAP)
    mean = lax.concatenate([jnp.where(core == 0, half, other), jnp.where(core == 0, other, half)], 0)

    qt = q_init.T
    pt = None
    for step in range(ITERS):
        pt = dot(qt, mean, ((1,), (1,)))
        zt = dot(pt, mean, ((1,), (0,)))
        gram = dot(pt, pt, ((1,), (1,)))
        tot = sum_y(lax.concatenate([zt, jnp.pad(gram, ((0, 0), (0, 64)))], 1))
        zt, gram = tot[:, :512], tot[:, 512:576]
        lower = jnp.linalg.cholesky(gram)
        rhs = zt if step < ITERS - 1 else lax.concatenate([zt, pt], 1)
        sol = lax.linalg.triangular_solve(lower, rhs, left_side=True, lower=True)
        qt = sol[:, :512]
    pt = sol[:, 512:]
    approx = dot(pt, qt, ((0,), (0,)))
    new_error = (merged - approx)[None]
    return (input_grad, approx, new_error, qt.T)


def solution(mesh):
    fine = Mesh(mesh.devices.reshape(NX, NZ, NC, NY), ("x", "z", "core", "y"))
    every = P((*DP, "y"), None)
    in_specs = (every, every, P("y", None), P(DP, "y", None), P(), P())
    out_specs = (every, P("y", None), P(DP, "y", None), P())
    return jax.shard_map(body, mesh=fine, in_specs=in_specs, out_specs=out_specs, check_vma=False)
```

```python
import jax
import jax.numpy as jnp
from jax import lax
from jax.experimental import pallas as pl
from jax.experimental.pallas import tpu as pltpu
from jax.sharding import Mesh
from jax.sharding import PartitionSpec as P

ITERS = 2
NX, NZ, NC, NY = 4, 8, 2, 4
DP = ("x", "z", "core")
D, KVC, R, TOK = 4096, 512, 64, 512
ROWS = D // NY
HALF = ROWS // NC
COLS = KVC // 2
WIDE = KVC + 128
HI = lax.Precision.HIGHEST
f32, bf16 = jnp.float32, jnp.bfloat16
SWAP = [(0, 1), (1, 0)]
FLIP = [(i, i ^ 1) for i in range(NY)]
MIRROR = [(i, 3 - i) for i in range(NY)]
VMEM_LIMIT = 24 * 1024 * 1024


def params(**kw):
    return pltpu.CompilerParams(vmem_limit_bytes=VMEM_LIMIT, **kw)


def sds(shape, dtype=f32):
    return jax.ShapeDtypeStruct(shape, dtype)


def whole(shape):
    return pl.BlockSpec(shape, lambda *_: (0,) * len(shape))


def dot(a, b, dims):
    return lax.dot_general(a, b, (dims, ((), ())), precision=HI, preferred_element_type=f32)


NT = ((1,), (1,))
NN = ((1,), (0,))
TN = ((0,), (0,))


def inverse_lower(block):
    lane = lax.broadcasted_iota(jnp.int32, (8, 128), 1)
    sub = lax.broadcasted_iota(jnp.int32, (8, 128), 0)
    tiles = [
        jnp.where(lane < R, block[8 * i : 8 * i + 8], jnp.where(lane - R == sub + 8 * i, 1.0, 0.0))
        for i in range(8)
    ]
    for k in range(R):
        a, b = divmod(k, 8)
        row = tiles[a][b : b + 1, :]
        scale = lax.rsqrt(row[:, k : k + 1])
        row = row * scale
        for i in range(a, 8):
            col = tiles[i][:, k : k + 1] * scale
            new = tiles[i] - col * row
            if i == a:
                new = jnp.where(sub > b, new, jnp.where(sub == b, row, tiles[i]))
            tiles[i] = new
    return jnp.concatenate(tiles, axis=0)[:, R:]


def products(qt, half_ref, other_ref, p_ref, t_ref):
    z, g = [], []
    for n, ref in enumerate((half_ref, other_ref)):
        m = ref[...]
        p = dot(qt, m, NT)
        p_ref[n] = p
        z.append(dot(p, m, NN))
        g.append(dot(p, jnp.concatenate([p, jnp.zeros_like(p)], axis=0), NT))
    zt = z[0] + z[1]
    gram = g[0] + g[1]
    for s in range(NY):
        t_ref[s, :, :KVC] = zt
        t_ref[s, :, KVC:] = gram


def total(got_ref, lo, hi):
    return (got_ref[0, :, lo:hi] + got_ref[1, :, lo:hi]) + (got_ref[2, :, lo:hi] + got_ref[3, :, lo:hi])


def first_kernel(q_ref, half_ref, other_ref, t_ref, p_ref):
    products(q_ref[...], half_ref, other_ref, p_ref, t_ref)


def next_kernel(got_ref, half_ref, other_ref, t_ref, p_ref):
    inv = inverse_lower(total(got_ref, KVC, WIDE))
    qt = dot(inv, total(got_ref, 0, KVC), NN)
    products(qt, half_ref, other_ref, p_ref, t_ref)


def first(qt, half, other):
    return pl.pallas_call(
        first_kernel, name="first", out_shape=(sds((NY, R, WIDE)), sds((2, R, HALF))), compiler_params=params()
    )(qt, half, other)


def following(got, half, other):
    return pl.pallas_call(
        next_kernel, name="following", out_shape=(sds((NY, R, WIDE)), sds((2, R, HALF))), compiler_params=params()
    )(got, half, other)


def last_kernel(core_ref, got_ref, p_ref, merged_ref, approx_ref, err_ref, q_ref, ph):
    @pl.when(pl.program_id(0) == 0)
    def _():
        inv = inverse_lower(total(got_ref, KVC, WIDE))
        q_ref[...] = dot(inv, total(got_ref, 0, KVC), NN)
        for n in range(2):
            p = dot(inv, p_ref[n], NN)
            ph[2 * n] = p[:, : HALF // 2]
            ph[2 * n + 1] = p[:, HALF // 2 :]

    approx = dot(ph[pl.program_id(0)], q_ref[...], TN)
    approx_ref[...] = approx
    err_ref[...] = merged_ref[...] - approx


def last(core, got, p, merged):
    rows = HALF // 2
    place = pl.BlockSpec((rows, KVC), lambda i, c: ((i + 2 * c[0]) % 4, 0))
    return pl.pallas_call(
        last_kernel,
        name="last",
        grid_spec=pltpu.PrefetchScalarGridSpec(
            num_scalar_prefetch=1,
            grid=(4,),
            in_specs=[whole((NY, R, WIDE)), whole((2, R, HALF)), place],
            out_specs=[place, place, whole((R, KVC))],
            scratch_shapes=[pltpu.VMEM((4, R, rows), f32)],
        ),
        out_shape=(sds((ROWS, KVC)), sds((ROWS, KVC)), sds((R, KVC))),
        compiler_params=params(),
    )(core, got, p, merged)


def merge_kernel(at_ref, s_ref, pa, va, wa, pb, vb, wb, e_ref, merged_ref, give_ref):
    def add(p, v, w):
        return p[0].astype(f32) + v[...].astype(f32) + w[...].astype(f32)

    scale = s_ref[0]
    left = e_ref[:, :COLS] + scale * add(pa, va, wa)
    right = e_ref[:, COLS:] + scale * add(pb, vb, wb)
    merged_ref[:, :COLS] = left
    merged_ref[:, COLS:] = right

    @pl.when(pl.program_id(0) < 2)
    def _():
        give_ref[:, :COLS] = left.astype(bf16)
        give_ref[:, COLS:] = right.astype(bf16)


def merge(at, scale, pa, va, wa, pb, vb, wb, error):
    rows = HALF // 2

    def block(i, a):
        return (i + 2 * (1 - a[1])) % 4

    own = pl.BlockSpec((1, rows, COLS), lambda i, a, s: (a[0], block(i, a), 0))
    got = pl.BlockSpec((rows, COLS), lambda i, a, s: (block(i, a), 0))
    place = pl.BlockSpec((rows, KVC), lambda i, a, s: (block(i, a), 0))
    give = pl.BlockSpec((rows, KVC), lambda i, a, s: (jnp.minimum(i, 1), 0))
    return pl.pallas_call(
        merge_kernel,
        name="merge",
        grid_spec=pltpu.PrefetchScalarGridSpec(
            num_scalar_prefetch=2,
            grid=(4,),
            in_specs=[own, got, got, own, got, got, place],
            out_specs=[place, give],
        ),
        out_shape=(sds((ROWS, KVC)), sds((HALF, KVC), bf16)),
        compiler_params=params(),
    )(at, scale, pa, va, wa, pb, vb, wb, error)


def input_grad_kernel(at_ref, cot_ref, w0, w1, w2, w3, other_ref, out_ref):
    for g in range(2 * NY):

        @pl.when(pl.program_id(0) == g)
        def _(g=g):
            w = (w0, w1, w2, w3)[g][...] if g < NY else other_ref[g - NY]
            out_ref[...] = lax.dot_general(
                cot_ref[...], w, (NT, ((), ())), preferred_element_type=f32
            ).astype(bf16)


def input_grad_of(at, cot, pieces, other):
    piece = whole((HALF, KVC))
    return pl.pallas_call(
        input_grad_kernel,
        name="input_grad",
        grid_spec=pltpu.PrefetchScalarGridSpec(
            num_scalar_prefetch=1,
            grid=(2 * NY,),
            in_specs=[whole((TOK, KVC)), piece, piece, piece, piece, whole((NY, HALF, KVC))],
            out_specs=pl.BlockSpec((TOK, HALF), lambda i, a: (0, a[i])),
        ),
        out_shape=sds((TOK, D), bf16),
        compiler_params=params(),
        cost_estimate=pl.CostEstimate(flops=2 * TOK * D * KVC, bytes_accessed=9 << 20, transcendentals=0),
    )(at, cot, *pieces, other)


def scatter_y(acts, cot, y):
    flip, mirror = y ^ 1, 3 - y
    out = []
    parts = [
        jnp.einsum("tr,tk->rk", acts, cot[:, n * COLS : (n + 1) * COLS], preferred_element_type=f32)
        .astype(bf16)
        .reshape(NY, ROWS, COLS)
        for n in range(2)
    ]
    plans = ((FLIP, MIRROR, flip, mirror), (MIRROR, FLIP, mirror, flip))

    def take(n, index):
        return lax.dynamic_index_in_dim(parts[n], index, 0, keepdims=False)

    firsts = [lax.ppermute(take(n, 3 - (y ^ 1)), "y", plans[n][0]) for n in range(2)]
    seconds = [lax.ppermute(take(n, plans[n][2]), "y", plans[n][0]) for n in range(2)]
    for n in range(2):
        onward = (firsts[n].astype(f32) + take(n, plans[n][3]).astype(f32)).astype(bf16)
        out += [parts[n], seconds[n], lax.ppermute(onward, "y", plans[n][1])]
    return out


def everyone(t, axis, n):
    return lax.all_to_all(jnp.broadcast_to(t, (n, *t.shape)), axis, 0, 0, tiled=True)


def body(acts, cotangent, weight, error_buf, q_init, inv_scale):
    y, core = lax.axis_index("y"), lax.axis_index("core")
    terms = scatter_y(acts, cotangent, y)
    merged, give = merge(jnp.stack([y, core]), inv_scale[None], *terms, error_buf[0])

    give, weight = lax.optimization_barrier((give, weight))
    keep = lax.dynamic_slice_in_dim(merged, core * HALF, HALF, 0)
    pair = keep + lax.ppermute(give, "core", SWAP).astype(f32)
    along_x = lax.all_to_all(pair.astype(bf16).reshape(NX, 128, KVC), "x", 0, 0, tiled=True)
    row = jnp.sum(along_x.astype(f32), axis=0)
    along_z = lax.all_to_all(row.reshape(NZ, 16, KVC), "z", 0, 0, tiled=True)
    rows = jnp.sum(along_z, axis=0) * (1.0 / (NX * NZ * NC))
    block = everyone(rows, "z", NZ).reshape(128, KVC)
    half = everyone(block, "x", NX).reshape(HALF, KVC)
    other = lax.ppermute(half, "core", SWAP)

    mine = lax.dynamic_slice_in_dim(weight, core * HALF, HALF, 0)
    pieces = [mine] + [
        lax.ppermute(mine, "y", [(i, (i + s) % NY) for i in range(NY)]) for s in range(1, NY)
    ]
    others = lax.ppermute(jnp.stack(pieces), "core", SWAP)
    source = (y - jnp.arange(NY)) % NY
    at = jnp.concatenate([2 * source + core, 2 * source + 1 - core])
    input_grad = input_grad_of(at, cotangent, pieces, others)

    t, p = first(q_init.T, half, other)
    for _ in range(ITERS - 1):
        t, p = following(lax.all_to_all(t, "y", 0, 0, tiled=True), half, other)
    approx, new_error, qt = last(core[None], lax.all_to_all(t, "y", 0, 0, tiled=True), p, merged)
    return (input_grad, approx, new_error[None], qt.T)


def solution(mesh):
    fine = Mesh(mesh.devices.reshape(NX, NZ, NC, NY), ("x", "z", "core", "y"))
    every = P((*DP, "y"), None)
    in_specs = (every, every, P("y", None), P(DP, "y", None), P(), P())
    out_specs = (every, P("y", None), P(DP, "y", None), P())
    return jax.shard_map(body, mesh=fine, in_specs=in_specs, out_specs=out_specs, check_vma=False)
```

```python
import jax
import jax.numpy as jnp
from jax import lax
from jax.experimental import pallas as pl
from jax.experimental.pallas import tpu as pltpu
from jax.sharding import Mesh
from jax.sharding import PartitionSpec as P

ITERS = 2
NX, NZ, NC, NY = 4, 8, 2, 4
DP = ("x", "z", "core")
D, KVC, R, TOK = 4096, 512, 64, 512
ROWS = D // NY
HALF = ROWS // NC
WIDE = KVC + 128
HI = lax.Precision.HIGHEST
f32, bf16 = jnp.float32, jnp.bfloat16
SWAP = [(0, 1), (1, 0)]
FLIP = [(i, i ^ 1) for i in range(NY)]
MIRROR = [(i, 3 - i) for i in range(NY)]
VMEM_LIMIT = 24 * 1024 * 1024


def params(**kw):
    return pltpu.CompilerParams(vmem_limit_bytes=VMEM_LIMIT, **kw)


def sds(shape, dtype=f32):
    return jax.ShapeDtypeStruct(shape, dtype)


def whole(shape):
    return pl.BlockSpec(shape, lambda *_: (0,) * len(shape))


def dot(a, b, dims):
    return lax.dot_general(a, b, (dims, ((), ())), precision=HI, preferred_element_type=f32)


NT = ((1,), (1,))
NN = ((1,), (0,))
TN = ((0,), (0,))


def inverse_lower(block):
    lane = lax.broadcasted_iota(jnp.int32, (8, 128), 1)
    sub = lax.broadcasted_iota(jnp.int32, (8, 128), 0)
    tiles = [
        jnp.where(lane < R, block[8 * i : 8 * i + 8], jnp.where(lane - R == sub + 8 * i, 1.0, 0.0))
        for i in range(8)
    ]
    for k in range(0, R, 2):
        a, b = divmod(k, 8)
        row0, row1 = tiles[a][b : b + 1, :], tiles[a][b + 1 : b + 2, :]
        cross = row0[:, k + 1 : k + 2]
        scale0 = lax.rsqrt(row0[:, k : k + 1])
        below = cross * scale0
        scale1 = lax.rsqrt(row1[:, k + 1 : k + 2] - below * below)
        row0 = row0 * scale0
        row1 = (row1 - below * row0) * scale1
        for i in range(a, 8):
            col0 = tiles[i][:, k : k + 1] * scale0
            col1 = (tiles[i][:, k + 1 : k + 2] - col0 * below) * scale1
            new = (tiles[i] - col0 * row0) - col1 * row1
            if i == a:
                new = jnp.where(sub > b + 1, new, tiles[i])
                new = jnp.where(sub == b, row0, jnp.where(sub == b + 1, row1, new))
            tiles[i] = new
    return jnp.concatenate(tiles, axis=0)[:, R:]


def products(qt, half_ref, other_ref, p_ref, t_ref):
    z, g = [], []
    for n, ref in enumerate((half_ref, other_ref)):
        m = ref[...]
        p = dot(qt, m, NT)
        p_ref[n] = p
        z.append(dot(p, m, NN))
        g.append(dot(p, jnp.concatenate([p, jnp.zeros_like(p)], axis=0), NT))
    zt = z[0] + z[1]
    gram = g[0] + g[1]
    for s in range(NY):
        t_ref[s, :, :KVC] = zt
        t_ref[s, :, KVC:] = gram


def total(got_ref, lo, hi):
    return (got_ref[0, :, lo:hi] + got_ref[1, :, lo:hi]) + (got_ref[2, :, lo:hi] + got_ref[3, :, lo:hi])


def first_kernel(q_ref, half_ref, other_ref, t_ref, p_ref):
    products(q_ref[...], half_ref, other_ref, p_ref, t_ref)


def next_kernel(got_ref, half_ref, other_ref, t_ref, p_ref):
    inv = inverse_lower(total(got_ref, KVC, WIDE))
    qt = dot(inv, total(got_ref, 0, KVC), NN)
    products(qt, half_ref, other_ref, p_ref, t_ref)


def first(qt, half, other):
    return pl.pallas_call(
        first_kernel, name="first", out_shape=(sds((NY, R, WIDE)), sds((2, R, HALF))), compiler_params=params()
    )(qt, half, other)


def following(got, half, other):
    return pl.pallas_call(
        next_kernel, name="following", out_shape=(sds((NY, R, WIDE)), sds((2, R, HALF))), compiler_params=params()
    )(got, half, other)


def last_kernel(core_ref, got_ref, p_ref, keep_ref, rest_ref, approx_ref, err_ref, q_ref, ph):
    i = pl.program_id(0)

    @pl.when(i == 0)
    def _():
        inv = inverse_lower(total(got_ref, KVC, WIDE))
        q_ref[...] = dot(inv, total(got_ref, 0, KVC), NN)
        for n in range(2):
            p = dot(inv, p_ref[n], NN)
            ph[2 * n] = p[:, : HALF // 2]
            ph[2 * n + 1] = p[:, HALF // 2 :]

    approx = dot(ph[i], q_ref[...], TN)
    approx_ref[...] = approx

    @pl.when(i < 2)
    def _():
        err_ref[...] = keep_ref[...] - approx

    @pl.when(i >= 2)
    def _():
        err_ref[...] = rest_ref[...] - approx


def last(core, got, p, keep, rest):
    rows = HALF // 2
    place = pl.BlockSpec((rows, KVC), lambda i, c: ((i + 2 * c[0]) % 4, 0))
    return pl.pallas_call(
        last_kernel,
        name="last",
        grid_spec=pltpu.PrefetchScalarGridSpec(
            num_scalar_prefetch=1,
            grid=(4,),
            in_specs=[
                whole((NY, R, WIDE)),
                whole((2, R, HALF)),
                pl.BlockSpec((rows, KVC), lambda i, c: (jnp.minimum(i, 1), 0)),
                pl.BlockSpec((rows, KVC), lambda i, c: (jnp.maximum(i - 2, 0), 0)),
            ],
            out_specs=[place, place, whole((R, KVC))],
            scratch_shapes=[pltpu.VMEM((4, R, rows), f32)],
        ),
        out_shape=(sds((ROWS, KVC)), sds((ROWS, KVC)), sds((R, KVC))),
        compiler_params=params(),
    )(core, got, p, keep, rest)


def input_grad_kernel(at_ref, cot_ref, w0, w1, w2, w3, *refs):
    out_ref = refs[-1]
    for g, w in enumerate((w0, w1, w2, w3)):

        @pl.when(pl.program_id(0) == g)
        def _(w=w):
            out_ref[...] = lax.dot_general(
                cot_ref[...], w[...], (NT, ((), ())), preferred_element_type=f32
            ).astype(bf16)


def input_grad_of(at, cot, pieces, before=None):
    piece = whole((HALF, KVC))
    extra = [] if before is None else [before]
    return pl.pallas_call(
        input_grad_kernel,
        name="input_grad",
        grid_spec=pltpu.PrefetchScalarGridSpec(
            num_scalar_prefetch=1,
            grid=(NY,),
            in_specs=[whole((TOK, KVC))] + [piece] * NY + [pl.BlockSpec(memory_space=pl.ANY) for _ in extra],
            out_specs=pl.BlockSpec((TOK, HALF), lambda i, a: (0, a[i])),
        ),
        out_shape=sds((TOK, D), bf16),
        input_output_aliases={} if before is None else {2 + NY: 0},
        compiler_params=params(),
        cost_estimate=pl.CostEstimate(flops=TOK * D * KVC, bytes_accessed=5 << 20, transcendentals=0),
    )(at, cot, *pieces, *extra)


def scatter_y(acts, cot, error, scale, y):
    def term(block, half):
        rows = lax.dynamic_slice(acts, (0, block * ROWS + half * HALF), (TOK, HALF))
        return jnp.einsum("tr,tk->rk", rows, cot, preferred_element_type=f32)

    near = (y ^ 1, y ^ 3)
    pairs = (FLIP, MIRROR)
    firsts = [lax.ppermute(term(y ^ 2, n).astype(bf16), "y", pairs[n]) for n in range(2)]
    seconds = [lax.ppermute(term(near[n], n).astype(bf16), "y", pairs[n]) for n in range(2)]
    mids = [lax.optimization_barrier(term(near[1 - n], n)) for n in range(2)]
    owns = [lax.optimization_barrier(error[n * HALF : (n + 1) * HALF] + scale * term(y, n)) for n in range(2)]
    onward = [
        lax.ppermute((firsts[n].astype(f32) + mids[n]).astype(bf16), "y", pairs[1 - n]) for n in range(2)
    ]
    bases = [lax.optimization_barrier(owns[n] + scale * seconds[n].astype(f32)) for n in range(2)]
    return [bases[n] + scale * onward[n].astype(f32) for n in range(2)]


def everyone(t, axis, n):
    return lax.all_to_all(jnp.broadcast_to(t, (n, *t.shape)), axis, 0, 0, tiled=True)


def body(acts, cotangent, weight, error_buf, q_init, inv_scale):
    y, core = lax.axis_index("y"), lax.axis_index("core")
    low, high = scatter_y(acts, cotangent, error_buf[0], inv_scale, y)
    keep = jnp.where(core == 0, low, high)
    rest = jnp.where(core == 0, high, low)

    give, weight = lax.optimization_barrier((rest.astype(bf16), weight))
    pair = keep + lax.ppermute(give, "core", SWAP).astype(f32)
    along_x = lax.all_to_all(pair.astype(bf16).reshape(NX, 128, KVC), "x", 0, 0, tiled=True)
    row = jnp.sum(along_x.astype(f32), axis=0)
    along_z = lax.all_to_all(row.reshape(NZ, 16, KVC), "z", 0, 0, tiled=True)
    rows = jnp.sum(along_z, axis=0) * (1.0 / (NX * NZ * NC))
    block = everyone(rows, "z", NZ).reshape(128, KVC)

    mine = lax.dynamic_slice_in_dim(weight, core * HALF, HALF, 0)
    pieces = [mine] + [
        lax.ppermute(mine, "y", [(i, (i + s) % NY) for i in range(NY)]) for s in range(1, NY)
    ]
    block, *pieces = lax.optimization_barrier((block, *pieces))

    half = everyone(block, "x", NX).reshape(HALF, KVC)
    other = lax.ppermute(half, "core", SWAP)
    other, *pieces = lax.optimization_barrier((other, *pieces))
    others = [lax.ppermute(piece, "core", SWAP) for piece in pieces]
    source = (y - jnp.arange(NY)) % NY

    t, p = first(q_init.T, half, other)
    input_grad = input_grad_of(2 * source + core, cotangent, pieces)
    for _ in range(ITERS - 1):
        got = lax.all_to_all(t, "y", 0, 0, tiled=True)
        got, input_grad = lax.optimization_barrier((got, input_grad))
        t, p = following(got, half, other)
    input_grad = input_grad_of(2 * source + 1 - core, cotangent, others, input_grad)
    approx, new_error, qt = last(core[None], lax.all_to_all(t, "y", 0, 0, tiled=True), p, keep, rest)
    return (input_grad, approx, new_error[None], qt.T)


def solution(mesh):
    fine = Mesh(mesh.devices.reshape(NX, NZ, NC, NY), ("x", "z", "core", "y"))
    every = P((*DP, "y"), None)
    in_specs = (every, every, P("y", None), P(DP, "y", None), P(), P())
    out_specs = (every, P("y", None), P(DP, "y", None), P())
    return jax.shard_map(body, mesh=fine, in_specs=in_specs, out_specs=out_specs, check_vma=False)
```

```python
import jax
import jax.numpy as jnp
from jax import lax
from jax.experimental import pallas as pl
from jax.experimental.pallas import tpu as pltpu
from jax.sharding import Mesh
from jax.sharding import PartitionSpec as P

ITERS = 2
NX, NZ, NC, NY = 4, 8, 2, 4
DP = ("x", "z", "core")
D, KVC, R, TOK = 4096, 512, 64, 512
ROWS = D // NY
HALF = ROWS // NC
WIDE = KVC + 128
HI = lax.Precision.HIGHEST
f32, bf16 = jnp.float32, jnp.bfloat16
SWAP = [(0, 1), (1, 0)]
FLIP = [(i, i ^ 1) for i in range(NY)]
MIRROR = [(i, 3 - i) for i in range(NY)]


def params(room):
    return pltpu.CompilerParams(vmem_limit_bytes=64 * 1024 * 1024 - room)


def sds(shape, dtype=f32):
    return jax.ShapeDtypeStruct(shape, dtype)


def whole(shape):
    return pl.BlockSpec(shape, lambda *_: (0,) * len(shape))


def dot(a, b, dims):
    return lax.dot_general(a, b, (dims, ((), ())), precision=HI, preferred_element_type=f32)


NT = ((1,), (1,))
NN = ((1,), (0,))
TN = ((0,), (0,))


def inverse_lower(block):
    lane = lax.broadcasted_iota(jnp.int32, (8, 128), 1)
    sub = lax.broadcasted_iota(jnp.int32, (8, 128), 0)
    tiles = [
        jnp.where(lane < R, block[8 * i : 8 * i + 8], jnp.where(lane - R == sub + 8 * i, 1.0, 0.0))
        for i in range(8)
    ]

    def spread_row(t, r):
        return jnp.broadcast_to(t[r : r + 1, :], (8, 128))

    for a in range(8):
        cols = {
            i: [jnp.broadcast_to(tiles[i][:, 8 * a + j : 8 * a + j + 1], (8, 128)) for j in range(8)]
            for i in range(a, 8)
        }
        for j in range(8):
            scale = lax.rsqrt(spread_row(cols[a][j], j))
            row = spread_row(tiles[a], j) * scale
            heads = [spread_row(cols[a][m], j) * scale for m in range(j + 1, 8)]
            for i in range(a, 8):
                c = cols[i][j] * scale
                if i == a:
                    tiles[i] = jnp.where(sub == j, row, tiles[i] - jnp.where(sub > j, c, 0.0) * row)
                else:
                    tiles[i] = tiles[i] - c * row
                for n, m in enumerate(range(j + 1, 8)):
                    cols[i][m] = cols[i][m] - c * heads[n]
    return jnp.concatenate(tiles, axis=0)[:, R:]


def products(qt, mean_refs, p_ref, t_hbm, t_ref, sems):
    z, g = [], []
    for n, ref in enumerate(mean_refs):
        m = ref[...]
        p = dot(qt, m, NT)
        p_ref[n] = p
        z.append(dot(p, m, NN))
        g.append(dot(p, jnp.concatenate([p, jnp.zeros_like(p)], axis=0), NT))
    t_ref[:, :KVC] = z[0] + z[1]
    t_ref[:, KVC:] = g[0] + g[1]
    copies = [pltpu.make_async_copy(t_ref, t_hbm.at[s], sems.at[s]) for s in range(NY)]
    for copy in copies:
        copy.start()
    for copy in copies:
        copy.wait()


def total(got_ref, lo, hi):
    return (got_ref[0, :, lo:hi] + got_ref[1, :, lo:hi]) + (got_ref[2, :, lo:hi] + got_ref[3, :, lo:hi])


def first_kernel(q_ref, half_ref, other_ref, t_hbm, p_ref, t_ref, sems):
    products(q_ref[...], (half_ref, other_ref), p_ref, t_hbm, t_ref, sems)


def next_kernel(got_ref, half_hbm, other_hbm, t_hbm, p_ref, half_ref, other_ref, t_ref, sems, in_sems):
    copies = [
        pltpu.make_async_copy(half_hbm, half_ref, in_sems.at[0]),
        pltpu.make_async_copy(other_hbm, other_ref, in_sems.at[1]),
    ]
    for copy in copies:
        copy.start()
    inv = inverse_lower(total(got_ref, KVC, WIDE))
    qt = dot(inv, total(got_ref, 0, KVC), NN)
    for copy in copies:
        copy.wait()
    products(qt, (half_ref, other_ref), p_ref, t_hbm, t_ref, sems)


IN_HBM = pl.BlockSpec(memory_space=pltpu.HBM)
IN_VMEM = pl.BlockSpec(memory_space=pltpu.VMEM)


def first(qt, half, other):
    return pl.pallas_call(
        first_kernel,
        name="first",
        in_specs=[IN_VMEM, IN_VMEM, IN_VMEM],
        out_specs=[IN_HBM, IN_VMEM],
        out_shape=(sds((NY, R, WIDE)), sds((2, R, HALF))),
        scratch_shapes=[pltpu.VMEM((R, WIDE), f32), pltpu.SemaphoreType.DMA((NY,))],
        compiler_params=params(3400 << 10),
    )(qt, half, other)


def following(got, half, other):
    return pl.pallas_call(
        next_kernel,
        name="following",
        in_specs=[IN_VMEM, IN_HBM, IN_HBM],
        out_specs=[IN_HBM, IN_VMEM],
        out_shape=(sds((NY, R, WIDE)), sds((2, R, HALF))),
        scratch_shapes=[
            pltpu.VMEM((HALF, KVC), f32),
            pltpu.VMEM((HALF, KVC), f32),
            pltpu.VMEM((R, WIDE), f32),
            pltpu.SemaphoreType.DMA((NY,)),
            pltpu.SemaphoreType.DMA((2,)),
        ],
        compiler_params=params(1300 << 10),
    )(got, half, other)


def last_kernel(core_ref, got_ref, p_ref, keep_hbm, rest_hbm, approx_ref, err_ref, q_ref, ph, merged, sems):
    i = pl.program_id(0)
    copies = [
        pltpu.make_async_copy(keep_hbm, merged.at[0], sems.at[0]),
        pltpu.make_async_copy(rest_hbm, merged.at[1], sems.at[1]),
    ]

    @pl.when(i == 0)
    def _():
        for copy in copies:
            copy.start()
        inv = inverse_lower(total(got_ref, KVC, WIDE))
        q_ref[...] = dot(inv, total(got_ref, 0, KVC), NN)
        for n in range(2):
            p = dot(inv, p_ref[n], NN)
            ph[2 * n] = p[:, : HALF // 2]
            ph[2 * n + 1] = p[:, HALF // 2 :]
        for copy in copies:
            copy.wait()

    rows = HALF // 2
    approx = dot(ph[i], q_ref[...], TN)
    approx_ref[...] = approx
    err_ref[...] = merged[i // 2, pl.ds(pl.multiple_of((i % 2) * rows, rows), rows), :] - approx


def last(core, got, p, keep, rest):
    rows = HALF // 2
    place = pl.BlockSpec((rows, KVC), lambda i, c: ((i + 2 * c[0]) % 4, 0))
    return pl.pallas_call(
        last_kernel,
        name="last",
        grid_spec=pltpu.PrefetchScalarGridSpec(
            num_scalar_prefetch=1,
            grid=(4,),
            in_specs=[whole((NY, R, WIDE)), whole((2, R, HALF)), IN_HBM, IN_HBM],
            out_specs=[place, place, whole((R, KVC))],
            scratch_shapes=[
                pltpu.VMEM((4, R, rows), f32),
                pltpu.VMEM((2, HALF, KVC), f32),
                pltpu.SemaphoreType.DMA((2,)),
            ],
        ),
        out_shape=(sds((ROWS, KVC)), sds((ROWS, KVC)), sds((R, KVC))),
        compiler_params=params(1300 << 10),
    )(core, got, p, keep, rest)


def input_grad_kernel(at_ref, cot_ref, w0, w1, w2, w3, *refs):
    out_ref = refs[-1]
    for g, w in enumerate((w0, w1, w2, w3)):

        @pl.when(pl.program_id(0) == g)
        def _(w=w):
            out_ref[...] = lax.dot_general(
                cot_ref[...], w[...], (NT, ((), ())), preferred_element_type=f32
            ).astype(bf16)


def input_grad_of(at, cot, pieces, before=None):
    piece = whole((HALF, KVC))
    extra = [] if before is None else [before]
    return pl.pallas_call(
        input_grad_kernel,
        name="input_grad",
        grid_spec=pltpu.PrefetchScalarGridSpec(
            num_scalar_prefetch=1,
            grid=(NY,),
            in_specs=[whole((TOK, KVC))] + [piece] * NY + [pl.BlockSpec(memory_space=pl.ANY) for _ in extra],
            out_specs=pl.BlockSpec((TOK, HALF), lambda i, a: (0, a[i])),
        ),
        out_shape=sds((TOK, D), bf16),
        input_output_aliases={} if before is None else {2 + NY: 0},
        compiler_params=params(4 << 20),
        cost_estimate=pl.CostEstimate(flops=TOK * D * KVC, bytes_accessed=5 << 20, transcendentals=0),
    )(at, cot, *pieces, *extra)


def scatter_y(acts, cot, error, scale, y):
    def term(rows):
        return jnp.einsum("tr,tk->rk", rows, cot, preferred_element_type=f32).astype(bf16)

    near = (y ^ 1, y ^ 3)
    pairs = (FLIP, MIRROR)
    across = term(lax.dynamic_slice(acts, (0, (y ^ 2) * ROWS), (TOK, ROWS)))
    across, acts = lax.optimization_barrier((across, acts))
    firsts = [lax.ppermute(across[n * HALF : (n + 1) * HALF], "y", pairs[n]) for n in range(2)]
    terms = lax.optimization_barrier(term(acts)).reshape(NY, 2, HALF, KVC)

    def take(block, n):
        return lax.dynamic_slice(terms, (block, n, 0, 0), (1, 1, HALF, KVC)).reshape(HALF, KVC)

    seconds = [lax.ppermute(take(near[n], n), "y", pairs[n]) for n in range(2)]
    onward = [
        lax.ppermute((firsts[n].astype(f32) + take(near[1 - n], n).astype(f32)).astype(bf16), "y", pairs[1 - n])
        for n in range(2)
    ]
    owns = [error[n * HALF : (n + 1) * HALF] + scale * take(y, n).astype(f32) for n in range(2)]
    bases = [lax.optimization_barrier(owns[n] + scale * seconds[n].astype(f32)) for n in range(2)]
    return [bases[n] + scale * onward[n].astype(f32) for n in range(2)]


def everyone(t, axis, n):
    return lax.all_to_all(jnp.broadcast_to(t, (n, *t.shape)), axis, 0, 0, tiled=True)


def body(acts, cotangent, weight, error_buf, q_init, inv_scale):
    y, core = lax.axis_index("y"), lax.axis_index("core")
    low, high = scatter_y(acts, cotangent, error_buf[0], inv_scale, y)
    keep = jnp.where(core == 0, low, high)
    rest = jnp.where(core == 0, high, low)

    give, weight = lax.optimization_barrier((rest.astype(bf16), weight))
    pair = (keep + lax.ppermute(give, "core", SWAP).astype(f32)) * (1.0 / (NX * NZ * NC))
    along_x = lax.all_to_all(pair.astype(bf16).reshape(NX, 128, KVC), "x", 0, 0, tiled=True)
    mine = lax.dynamic_slice_in_dim(weight, core * HALF, HALF, 0)
    pieces = [mine] + [
        lax.ppermute(mine, "y", [(i, (i + s) % NY) for i in range(NY)]) for s in range(1, NY)
    ]
    along_x, pieces[1], pieces[3] = lax.optimization_barrier((along_x, pieces[1], pieces[3]))
    row = jnp.sum(along_x.astype(f32), axis=0).astype(bf16)
    along_z = lax.all_to_all(row.reshape(NZ, 16, KVC), "z", 0, 0, tiled=True)
    along_z, pieces[2] = lax.optimization_barrier((along_z, pieces[2]))
    rows = jnp.sum(along_z.astype(f32), axis=0)
    block = everyone(rows, "z", NZ).reshape(128, KVC)
    half = everyone(block, "x", NX).reshape(HALF, KVC)
    other = lax.ppermute(half, "core", SWAP)
    others = [lax.ppermute(piece, "core", SWAP) for piece in pieces]
    source = (y - jnp.arange(NY)) % NY

    t, p = first(q_init.T, half, other)
    input_grad = input_grad_of(2 * source + core, cotangent, pieces)
    for _ in range(ITERS - 1):
        got = lax.all_to_all(t, "y", 0, 0, tiled=True)
        got, input_grad = lax.optimization_barrier((got, input_grad))
        t, p = following(got, half, other)
    input_grad = input_grad_of(2 * source + 1 - core, cotangent, others, input_grad)
    approx, new_error, qt = last(core[None], lax.all_to_all(t, "y", 0, 0, tiled=True), p, keep, rest)
    return (input_grad, approx, new_error[None], qt.T)


def solution(mesh):
    fine = Mesh(mesh.devices.reshape(NX, NZ, NC, NY), ("x", "z", "core", "y"))
    every = P((*DP, "y"), None)
    in_specs = (every, every, P("y", None), P(DP, "y", None), P(), P())
    out_specs = (every, P("y", None), P(DP, "y", None), P())
    return jax.shard_map(body, mesh=fine, in_specs=in_specs, out_specs=out_specs, check_vma=False)
```

```python
import jax
import jax.numpy as jnp
from jax import lax
from jax.experimental import pallas as pl
from jax.experimental.pallas import tpu as pltpu
from jax.sharding import Mesh
from jax.sharding import PartitionSpec as P

ITERS = 2
NX, NZ, NC, NY = 4, 8, 2, 4
DP = ("x", "z", "core")
D, KVC, R, TOK = 4096, 512, 64, 512
ROWS = D // NY
HALF = ROWS // NC
WIDE = KVC + 128
HI = lax.Precision.HIGHEST
f32, bf16 = jnp.float32, jnp.bfloat16
SWAP = [(0, 1), (1, 0)]
FLIP = [(i, i ^ 1) for i in range(NY)]
MIRROR = [(i, 3 - i) for i in range(NY)]


def params(room):
    return pltpu.CompilerParams(vmem_limit_bytes=64 * 1024 * 1024 - room)


def sds(shape, dtype=f32):
    return jax.ShapeDtypeStruct(shape, dtype)


def whole(shape):
    return pl.BlockSpec(shape, lambda *_: (0,) * len(shape))


def dot(a, b, dims):
    return lax.dot_general(a, b, (dims, ((), ())), precision=HI, preferred_element_type=f32)


NT = ((1,), (1,))
NN = ((1,), (0,))
TN = ((0,), (0,))


def inverse_lower(block):
    lane = lax.broadcasted_iota(jnp.int32, (8, 128), 1)
    sub = lax.broadcasted_iota(jnp.int32, (8, 128), 0)
    tiles = [
        jnp.where(lane < R, block[8 * i : 8 * i + 8], jnp.where(lane - R == sub + 8 * i, 1.0, 0.0))
        for i in range(8)
    ]

    def spread_row(t, r):
        return jnp.broadcast_to(t[r : r + 1, :], (8, 128))

    for a in range(8):
        cols = {
            i: [jnp.broadcast_to(tiles[i][:, 8 * a + j : 8 * a + j + 1], (8, 128)) for j in range(8)]
            for i in range(a, 8)
        }
        for j in range(8):
            scale = lax.rsqrt(spread_row(cols[a][j], j))
            row = spread_row(tiles[a], j) * scale
            heads = [spread_row(cols[a][m], j) * scale for m in range(j + 1, 8)]
            for i in range(a, 8):
                c = cols[i][j] * scale
                if i == a:
                    tiles[i] = jnp.where(sub == j, row, tiles[i] - jnp.where(sub > j, c, 0.0) * row)
                else:
                    tiles[i] = tiles[i] - c * row
                for n, m in enumerate(range(j + 1, 8)):
                    cols[i][m] = cols[i][m] - c * heads[n]
    return jnp.concatenate(tiles, axis=0)[:, R:]


def products(qt, mean_refs, p_ref, t_hbm, t_ref, sems):
    z, g = [], []
    for n, ref in enumerate(mean_refs):
        m = ref[...]
        p = dot(qt, m, NT)
        p_ref[n] = p
        z.append(dot(p, m, NN))
        g.append(dot(p, jnp.concatenate([p, jnp.zeros_like(p)], axis=0), NT))
    t_ref[:, :KVC] = z[0] + z[1]
    t_ref[:, KVC:] = g[0] + g[1]
    copies = [pltpu.make_async_copy(t_ref, t_hbm.at[s], sems.at[s]) for s in range(NY)]
    for copy in copies:
        copy.start()
    for copy in copies:
        copy.wait()


def total(got_ref, lo, hi):
    return (got_ref[0, :, lo:hi] + got_ref[1, :, lo:hi]) + (got_ref[2, :, lo:hi] + got_ref[3, :, lo:hi])


def first_kernel(q_ref, half_ref, other_ref, t_hbm, p_ref, t_ref, sems):
    products(q_ref[...], (half_ref, other_ref), p_ref, t_hbm, t_ref, sems)


def next_kernel(got_ref, half_hbm, other_hbm, t_hbm, p_ref, half_ref, other_ref, t_ref, sems, in_sems):
    copies = [
        pltpu.make_async_copy(half_hbm, half_ref, in_sems.at[0]),
        pltpu.make_async_copy(other_hbm, other_ref, in_sems.at[1]),
    ]
    for copy in copies:
        copy.start()
    inv = inverse_lower(total(got_ref, KVC, WIDE))
    qt = dot(inv, total(got_ref, 0, KVC), NN)
    for copy in copies:
        copy.wait()
    products(qt, (half_ref, other_ref), p_ref, t_hbm, t_ref, sems)


IN_HBM = pl.BlockSpec(memory_space=pltpu.HBM)
IN_VMEM = pl.BlockSpec(memory_space=pltpu.VMEM)


def first(qt, half, other):
    return pl.pallas_call(
        first_kernel,
        name="first",
        in_specs=[IN_VMEM, IN_VMEM, IN_VMEM],
        out_specs=[IN_HBM, IN_VMEM],
        out_shape=(sds((NY, R, WIDE)), sds((2, R, HALF))),
        scratch_shapes=[pltpu.VMEM((R, WIDE), f32), pltpu.SemaphoreType.DMA((NY,))],
        compiler_params=params(40 << 20),
    )(qt, half, other)


def following(got, half, other):
    return pl.pallas_call(
        next_kernel,
        name="following",
        in_specs=[IN_VMEM, IN_HBM, IN_HBM],
        out_specs=[IN_HBM, IN_VMEM],
        out_shape=(sds((NY, R, WIDE)), sds((2, R, HALF))),
        scratch_shapes=[
            pltpu.VMEM((HALF, KVC), f32),
            pltpu.VMEM((HALF, KVC), f32),
            pltpu.VMEM((R, WIDE), f32),
            pltpu.SemaphoreType.DMA((NY,)),
            pltpu.SemaphoreType.DMA((2,)),
        ],
        compiler_params=params(1300 << 10),
    )(got, half, other)


def last_kernel(core_ref, got_ref, p_ref, keep_hbm, rest_hbm, approx_ref, err_ref, q_ref, ph, merged, sems):
    i = pl.program_id(0)
    copies = [
        pltpu.make_async_copy(keep_hbm, merged.at[0], sems.at[0]),
        pltpu.make_async_copy(rest_hbm, merged.at[1], sems.at[1]),
    ]

    @pl.when(i == 0)
    def _():
        for copy in copies:
            copy.start()
        inv = inverse_lower(total(got_ref, KVC, WIDE))
        q_ref[...] = dot(inv, total(got_ref, 0, KVC), NN)
        for n in range(2):
            p = dot(inv, p_ref[n], NN)
            ph[2 * n] = p[:, : HALF // 2]
            ph[2 * n + 1] = p[:, HALF // 2 :]
        for copy in copies:
            copy.wait()

    rows = HALF // 2
    approx = dot(ph[i], q_ref[...], TN)
    approx_ref[...] = approx
    err_ref[...] = merged[i // 2, pl.ds(pl.multiple_of((i % 2) * rows, rows), rows), :] - approx


def last(core, got, p, keep, rest):
    rows = HALF // 2
    place = pl.BlockSpec((rows, KVC), lambda i, c: ((i + 2 * c[0]) % 4, 0))
    return pl.pallas_call(
        last_kernel,
        name="last",
        grid_spec=pltpu.PrefetchScalarGridSpec(
            num_scalar_prefetch=1,
            grid=(4,),
            in_specs=[whole((NY, R, WIDE)), whole((2, R, HALF)), IN_HBM, IN_HBM],
            out_specs=[place, place, whole((R, KVC))],
            scratch_shapes=[
                pltpu.VMEM((4, R, rows), f32),
                pltpu.VMEM((2, HALF, KVC), f32),
                pltpu.SemaphoreType.DMA((2,)),
            ],
        ),
        out_shape=(sds((ROWS, KVC)), sds((ROWS, KVC)), sds((R, KVC))),
        compiler_params=params(1300 << 10),
    )(core, got, p, keep, rest)


def input_grad_kernel(at_ref, cot_ref, w0, w1, w2, w3, *refs):
    out_ref = refs[-1]
    for g, w in enumerate((w0, w1, w2, w3)):

        @pl.when(pl.program_id(0) == g)
        def _(w=w):
            out_ref[...] = lax.dot_general(
                cot_ref[...], w[...], (NT, ((), ())), preferred_element_type=f32
            ).astype(bf16)


def input_grad_of(at, cot, pieces, before=None):
    piece = whole((HALF, KVC))
    extra = [] if before is None else [before]
    return pl.pallas_call(
        input_grad_kernel,
        name="input_grad",
        grid_spec=pltpu.PrefetchScalarGridSpec(
            num_scalar_prefetch=1,
            grid=(NY,),
            in_specs=[whole((TOK, KVC))] + [piece] * NY + [pl.BlockSpec(memory_space=pl.ANY) for _ in extra],
            out_specs=pl.BlockSpec((TOK, HALF), lambda i, a: (0, a[i])),
        ),
        out_shape=sds((TOK, D), bf16),
        input_output_aliases={} if before is None else {2 + NY: 0},
        compiler_params=params(4 << 20),
        cost_estimate=pl.CostEstimate(flops=TOK * D * KVC, bytes_accessed=5 << 20, transcendentals=0),
    )(at, cot, *pieces, *extra)


def scatter_y(acts, cot, error, scale, y):
    def term(rows):
        return jnp.einsum("tr,tk->rk", rows, cot, preferred_element_type=f32).astype(bf16)

    near = (y ^ 1, y ^ 3)
    pairs = (FLIP, MIRROR)
    across = term(lax.dynamic_slice(acts, (0, (y ^ 2) * ROWS), (TOK, ROWS)))
    across, acts = lax.optimization_barrier((across, acts))
    firsts = [lax.ppermute(across[n * HALF : (n + 1) * HALF], "y", pairs[n]) for n in range(2)]
    terms = lax.optimization_barrier(term(acts)).reshape(NY, 2, HALF, KVC)

    def take(block, n):
        return lax.dynamic_slice(terms, (block, n, 0, 0), (1, 1, HALF, KVC)).reshape(HALF, KVC)

    seconds = [lax.ppermute(take(near[n], n), "y", pairs[n]) for n in range(2)]
    sent = []
    for n in range(2):
        sent.append((firsts[n].astype(f32) + take(near[1 - n], n).astype(f32)).astype(bf16))
        if n == 0:
            firsts[1], _ = lax.optimization_barrier((firsts[1], sent[0]))
    onward = [lax.ppermute(sent[n], "y", pairs[1 - n]) for n in range(2)]
    terms, error, _ = lax.optimization_barrier((terms, error, sent[1]))
    bases = [
        error[n * HALF : (n + 1) * HALF] + scale * (take(y, n).astype(f32) + seconds[n].astype(f32))
        for n in range(2)
    ]
    bases = [lax.optimization_barrier(base) for base in bases]
    return [bases[n] + scale * onward[n].astype(f32) for n in range(2)]


def everyone(t, axis, n):
    return lax.all_to_all(jnp.broadcast_to(t, (n, *t.shape)), axis, 0, 0, tiled=True)


def body(acts, cotangent, weight, error_buf, q_init, inv_scale):
    y, core = lax.axis_index("y"), lax.axis_index("core")
    low, high = scatter_y(acts, cotangent, error_buf[0], inv_scale, y)
    keep = jnp.where(core == 0, low, high)
    rest = jnp.where(core == 0, high, low)

    pair = (keep + lax.ppermute(rest.astype(bf16), "core", SWAP).astype(f32)) * (1.0 / (NX * NZ * NC))
    along_x = lax.all_to_all(pair.astype(bf16).reshape(NX, 128, KVC), "x", 0, 0, tiled=True)
    row = jnp.sum(along_x.astype(f32), axis=0).astype(bf16)
    mine = lax.dynamic_slice_in_dim(weight, core * HALF, HALF, 0)
    row, mine = lax.optimization_barrier((row, mine))

    def turn(rows, s):
        return lax.ppermute(rows, "y", [(i, (i + s) % NY) for i in range(NY)])

    after, before = turn(mine, 1), turn(mine, 3)
    along_z = lax.all_to_all(row.reshape(NZ, 16, KVC), "z", 0, 0, tiled=True)
    along_z, after, before = lax.optimization_barrier((along_z, after, before))
    rows = jnp.sum(along_z.astype(f32), axis=0)
    rows, mine = lax.optimization_barrier((rows, mine))
    facing = turn(mine, 2)
    block = everyone(rows, "z", NZ).reshape(128, KVC)
    half = everyone(block, "x", NX).reshape(HALF, KVC)
    half, facing = lax.optimization_barrier((half, facing))
    pieces = [mine, after, facing, before]
    other = lax.ppermute(half, "core", SWAP)
    others = [lax.ppermute(piece, "core", SWAP) for piece in pieces]
    source = (y - jnp.arange(NY)) % NY

    t, p = first(q_init.T, half, other)
    input_grad = input_grad_of(2 * source + core, cotangent, pieces)
    for _ in range(ITERS - 1):
        got = lax.all_to_all(t, "y", 0, 0, tiled=True)
        got, input_grad = lax.optimization_barrier((got, input_grad))
        t, p = following(got, half, other)
    input_grad = input_grad_of(2 * source + 1 - core, cotangent, others, input_grad)
    approx, new_error, qt = last(core[None], lax.all_to_all(t, "y", 0, 0, tiled=True), p, keep, rest)
    return (input_grad, approx, new_error[None], qt.T)


def solution(mesh):
    fine = Mesh(mesh.devices.reshape(NX, NZ, NC, NY), ("x", "z", "core", "y"))
    every = P((*DP, "y"), None)
    in_specs = (every, every, P("y", None), P(DP, "y", None), P(), P())
    out_specs = (every, P("y", None), P(DP, "y", None), P())
    return jax.shard_map(body, mesh=fine, in_specs=in_specs, out_specs=out_specs, check_vma=False)
```

```python
import jax
import jax.numpy as jnp
from jax import lax
from jax.experimental import pallas as pl
from jax.experimental.pallas import tpu as pltpu
from jax.sharding import Mesh
from jax.sharding import PartitionSpec as P


ITERS = 2
NX, NZ, NC, NY = 4, 8, 2, 4
DP = ("x", "z", "core")
D, KVC, R, TOK = 4096, 512, 64, 512
ROWS = D // NY
HALF = ROWS // NC
WIDE = KVC + 128
HI = lax.Precision.HIGHEST
f32, bf16 = jnp.float32, jnp.bfloat16
SWAP = [(0, 1), (1, 0)]
FLIP = [(i, i ^ 1) for i in range(NY)]
MIRROR = [(i, 3 - i) for i in range(NY)]


def params(room):
    return pltpu.CompilerParams(vmem_limit_bytes=64 * 1024 * 1024 - room)


def sds(shape, dtype=f32):
    return jax.ShapeDtypeStruct(shape, dtype)


def whole(shape):
    return pl.BlockSpec(shape, lambda *_: (0,) * len(shape))


def dot(a, b, dims):
    return lax.dot_general(a, b, (dims, ((), ())), precision=HI, preferred_element_type=f32)


NT = ((1,), (1,))
NN = ((1,), (0,))
TN = ((0,), (0,))


def inverse_lower(block):
    lane = lax.broadcasted_iota(jnp.int32, (8, 128), 1)
    sub = lax.broadcasted_iota(jnp.int32, (8, 128), 0)
    tiles = [
        jnp.where(lane < R, block[8 * i : 8 * i + 8], jnp.where(lane - R == sub + 8 * i, 1.0, 0.0))
        for i in range(8)
    ]

    def spread_row(t, r):
        return jnp.broadcast_to(t[r : r + 1, :], (8, 128))

    for a in range(8):
        cols = {
            i: [jnp.broadcast_to(tiles[i][:, 8 * a + j : 8 * a + j + 1], (8, 128)) for j in range(8)]
            for i in range(a, 8)
        }
        for j in range(8):
            scale = lax.rsqrt(spread_row(cols[a][j], j))
            row = spread_row(tiles[a], j) * scale
            heads = [spread_row(cols[a][m], j) * scale for m in range(j + 1, 8)]
            for i in range(a, 8):
                c = cols[i][j] * scale
                if i == a:
                    tiles[i] = jnp.where(sub == j, row, tiles[i] - jnp.where(sub > j, c, 0.0) * row)
                else:
                    tiles[i] = tiles[i] - c * row
                for n, m in enumerate(range(j + 1, 8)):
                    cols[i][m] = cols[i][m] - c * heads[n]
    return jnp.concatenate(tiles, axis=0)[:, R:]


def products(qt, mean_refs, p_ref, t_ref):
    z, g = [], []
    for n, ref in enumerate(mean_refs):
        m = ref[...]
        p = dot(qt, m, NT)
        p_ref[n] = p
        z.append(dot(p, m, NN))
        g.append(dot(p, jnp.concatenate([p, jnp.zeros_like(p)], axis=0), NT))
    t_ref[:, :KVC] = z[0] + z[1]
    t_ref[:, KVC:] = g[0] + g[1]


def total(got, lo, hi):
    own, opposite, after, before = (ref[:, lo:hi] for ref in got)
    return (own + opposite) + (after + before)


def first_kernel(q_ref, half_ref, other_ref, t_ref, p_ref):
    products(q_ref[...], (half_ref, other_ref), p_ref, t_ref)


def next_kernel(g0, g1, g2, g3, half_hbm, other_hbm, t_ref, p_ref, half_ref, other_ref, sems):
    got = (g0, g1, g2, g3)
    copies = [
        pltpu.make_async_copy(half_hbm, half_ref, sems.at[0]),
        pltpu.make_async_copy(other_hbm, other_ref, sems.at[1]),
    ]
    for copy in copies:
        copy.start()
    inv = inverse_lower(total(got, KVC, WIDE))
    qt = dot(inv, total(got, 0, KVC), NN)
    for copy in copies:
        copy.wait()
    products(qt, (half_ref, other_ref), p_ref, t_ref)


IN_HBM = pl.BlockSpec(memory_space=pltpu.HBM)
IN_VMEM = pl.BlockSpec(memory_space=pltpu.VMEM)


def first(qt, half, other):
    return pl.pallas_call(
        first_kernel,
        name="first",
        in_specs=[IN_VMEM, IN_VMEM, IN_VMEM],
        out_specs=[IN_VMEM, IN_VMEM],
        out_shape=(sds((R, WIDE)), sds((2, R, HALF))),
        compiler_params=params(40 << 20),
    )(qt, half, other)


def following(got, half, other):
    return pl.pallas_call(
        next_kernel,
        name="following",
        in_specs=[IN_VMEM] * NY + [IN_HBM, IN_HBM],
        out_specs=[IN_VMEM, IN_VMEM],
        out_shape=(sds((R, WIDE)), sds((2, R, HALF))),
        scratch_shapes=[
            pltpu.VMEM((HALF, KVC), f32),
            pltpu.VMEM((HALF, KVC), f32),
            pltpu.SemaphoreType.DMA((2,)),
        ],
        compiler_params=params(1300 << 10),
    )(*got, half, other)


def last_kernel(core_ref, g0, g1, g2, g3, p_ref, keep_hbm, rest_hbm, approx_ref, err_ref, q_ref, ph, merged, sems):
    i = pl.program_id(0)
    got = (g0, g1, g2, g3)
    copies = [
        pltpu.make_async_copy(keep_hbm, merged.at[0], sems.at[0]),
        pltpu.make_async_copy(rest_hbm, merged.at[1], sems.at[1]),
    ]

    @pl.when(i == 0)
    def _():
        for copy in copies:
            copy.start()
        inv = inverse_lower(total(got, KVC, WIDE))
        q_ref[...] = dot(inv, total(got, 0, KVC), NN)
        for n in range(2):
            p = dot(inv, p_ref[n], NN)
            ph[2 * n] = p[:, : HALF // 2]
            ph[2 * n + 1] = p[:, HALF // 2 :]
        for copy in copies:
            copy.wait()

    rows = HALF // 2
    approx = dot(ph[i], q_ref[...], TN)
    approx_ref[...] = approx
    err_ref[...] = merged[i // 2, pl.ds(pl.multiple_of((i % 2) * rows, rows), rows), :] - approx


def last(core, got, p, keep, rest):
    rows = HALF // 2
    place = pl.BlockSpec((rows, KVC), lambda i, c: ((i + 2 * c[0]) % 4, 0))
    return pl.pallas_call(
        last_kernel,
        name="last",
        grid_spec=pltpu.PrefetchScalarGridSpec(
            num_scalar_prefetch=1,
            grid=(4,),
            in_specs=[whole((R, WIDE))] * NY + [whole((2, R, HALF)), IN_HBM, IN_HBM],
            out_specs=[place, place, whole((R, KVC))],
            scratch_shapes=[
                pltpu.VMEM((4, R, rows), f32),
                pltpu.VMEM((2, HALF, KVC), f32),
                pltpu.SemaphoreType.DMA((2,)),
            ],
        ),
        out_shape=(sds((ROWS, KVC)), sds((ROWS, KVC)), sds((R, KVC))),
        compiler_params=params(1300 << 10),
    )(core, *got, p, keep, rest)


def input_grad_kernel(at_ref, cot_ref, w0, w1, w2, w3, *refs):
    out_ref = refs[-1]
    for g, w in enumerate((w0, w1, w2, w3)):

        @pl.when(pl.program_id(0) == g)
        def _(w=w):
            out_ref[...] = lax.dot_general(
                cot_ref[...], w[...], (NT, ((), ())), preferred_element_type=f32
            ).astype(bf16)


def input_grad_of(at, cot, pieces, before=None):
    piece = whole((HALF, KVC))
    extra = [] if before is None else [before]
    return pl.pallas_call(
        input_grad_kernel,
        name="input_grad",
        grid_spec=pltpu.PrefetchScalarGridSpec(
            num_scalar_prefetch=1,
            grid=(NY,),
            in_specs=[whole((TOK, KVC))] + [piece] * NY + [pl.BlockSpec(memory_space=pl.ANY) for _ in extra],
            out_specs=pl.BlockSpec((TOK, HALF), lambda i, a: (0, a[i])),
        ),
        out_shape=sds((TOK, D), bf16),
        input_output_aliases={} if before is None else {2 + NY: 0},
        compiler_params=params(4 << 20),
        cost_estimate=pl.CostEstimate(flops=TOK * D * KVC, bytes_accessed=5 << 20, transcendentals=0),
    )(at, cot, *pieces, *extra)


def scatter_y(acts, cot, error, scale, y):
    def term(rows):
        return jnp.einsum("tr,tk->rk", rows, cot, preferred_element_type=f32).astype(bf16)

    near = (y ^ 1, y ^ 3)
    pairs = (FLIP, MIRROR)
    across = term(lax.dynamic_slice(acts, (0, (y ^ 2) * ROWS), (TOK, ROWS)))
    across, acts = lax.optimization_barrier((across, acts))
    firsts = [lax.ppermute(across[n * HALF : (n + 1) * HALF], "y", pairs[n]) for n in range(2)]
    terms = lax.optimization_barrier(term(acts)).reshape(NY, 2, HALF, KVC)

    def take(block, n):
        return lax.dynamic_slice(terms, (block, n, 0, 0), (1, 1, HALF, KVC)).reshape(HALF, KVC)

    seconds = [lax.ppermute(take(near[n], n), "y", pairs[n]) for n in range(2)]
    sent = []
    for n in range(2):
        sent.append((firsts[n].astype(f32) + take(near[1 - n], n).astype(f32)).astype(bf16))
        if n == 0:
            firsts[1], _ = lax.optimization_barrier((firsts[1], sent[0]))
    onward = [lax.ppermute(sent[n], "y", pairs[1 - n]) for n in range(2)]
    terms, error, _ = lax.optimization_barrier((terms, error, sent[1]))
    bases = [
        error[n * HALF : (n + 1) * HALF] + scale * (take(y, n).astype(f32) + seconds[n].astype(f32))
        for n in range(2)
    ]
    bases = [lax.optimization_barrier(base) for base in bases]
    return [bases[n] + scale * onward[n].astype(f32) for n in range(2)]


def turn(t, s):
    return lax.ppermute(t, "y", [(i, (i + s) % NY) for i in range(NY)])


def exchange(t):
    return [t] + [turn(t, s) for s in (2, 1, 3)]


def everyone(t, axis, n):
    return lax.all_to_all(jnp.broadcast_to(t, (n, *t.shape)), axis, 0, 0, tiled=True)


def body(acts, cotangent, weight, error_buf, q_init, inv_scale):
    y, core = lax.axis_index("y"), lax.axis_index("core")
    low, high = scatter_y(acts, cotangent, error_buf[0], inv_scale, y)
    keep = jnp.where(core == 0, low, high)
    rest = jnp.where(core == 0, high, low)

    pair = (keep + lax.ppermute(rest.astype(bf16), "core", SWAP).astype(f32)) * (1.0 / (NX * NZ * NC))
    along_x = lax.all_to_all(pair.astype(bf16).reshape(NX, 128, KVC), "x", 0, 0, tiled=True)
    row = jnp.sum(along_x.astype(f32), axis=0).astype(bf16)
    mine = lax.dynamic_slice_in_dim(weight, core * HALF, HALF, 0)
    row, mine = lax.optimization_barrier((row, mine))

    after, before = turn(mine, 1), turn(mine, 3)
    along_z = lax.all_to_all(row.reshape(NZ, 16, KVC), "z", 0, 0, tiled=True)
    along_z, after, before = lax.optimization_barrier((along_z, after, before))
    rows = jnp.sum(along_z.astype(f32), axis=0)
    rows, mine = lax.optimization_barrier((rows, mine))
    facing = turn(mine, 2)
    block = everyone(rows, "z", NZ).reshape(128, KVC)
    half = everyone(block, "x", NX).reshape(HALF, KVC)
    half, facing = lax.optimization_barrier((half, facing))
    pieces = [mine, after, facing, before]
    other = lax.ppermute(half, "core", SWAP)
    other, *pieces = lax.optimization_barrier((other, *pieces))
    others = [lax.ppermute(piece, "core", SWAP) for piece in pieces]
    source = (y - jnp.arange(NY)) % NY

    t, p = first(q_init.T, half, other)
    input_grad = input_grad_of(2 * source + core, cotangent, pieces)
    for _ in range(ITERS - 1):
        got = exchange(t)
        half, input_grad = lax.optimization_barrier((half, input_grad))
        t, p = following(got, half, other)
    input_grad = input_grad_of(2 * source + 1 - core, cotangent, others, input_grad)
    keep, input_grad = lax.optimization_barrier((keep, input_grad))
    approx, new_error, qt = last(core[None], exchange(t), p, keep, rest)
    return (input_grad, approx, new_error[None], qt.T)


def solution(mesh):
    fine = Mesh(mesh.devices.reshape(NX, NZ, NC, NY), ("x", "z", "core", "y"))
    every = P((*DP, "y"), None)
    in_specs = (every, every, P("y", None), P(DP, "y", None), P(), P())
    out_specs = (every, P("y", None), P(DP, "y", None), P())
    return jax.shard_map(body, mesh=fine, in_specs=in_specs, out_specs=out_specs, check_vma=False)
```
